1024 devices in a mesh: dp: 64 (over x, y), tensor: 8 (over z_lo, core), section: 2 (over z_hi).
Axes of the slice: x: 8, y: 8, z: 8 (z_hi: 2, z_lo: 4; z = z_hi * 4 + z_lo), core: 2. Of those that a mesh axis runs over, the one named last changes fastest.
Arguments:
- w_value: bfloat16 [8192, 1024], P(('dp', 'section'), 'tensor'), may hold values from -0.0625 to 0.0625
- hidden_new: bfloat16 [384, 4, 8192], P(('dp', 'section')), may hold values from -6 to 6
- query: bfloat16 [384, 4, 8192], P(('dp', 'section'), None, 'tensor'), may hold values from -240 to 240
- key_new: bfloat16 [384, 4, 1024], P(('dp', 'section'), None, 'tensor'), may hold values from -6 to 6
- key_cache: bfloat16 [384, 2048, 1024], P(('dp', 'section'), None, 'tensor'), may hold values from -6 to 6
- value_cache: bfloat16 [384, 2048, 1024], P(('dp', 'section'), None, 'tensor'), may hold values from -6 to 6
- cache_len: int32 [384], P(('dp', 'section')), may hold values from 512 to 2048, as said below
- sampled_rows: bfloat16 [16384, 8192], P(('dp', 'section')), may hold values from -6 to 6
- mb_map: int32 [128, 128], P(('dp', 'section')), may hold values from 0 to 127, each once within a row
- value_target: bfloat16 [16384, 1024], P(('dp', 'section'), 'tensor'), may hold values from -6 to 6
Outputs:
- attn_out: bfloat16 [384, 4, 8192], P(('dp', 'section'), None, 'tensor')
- grad_value: float32 [8192, 1024], P(('dp', 'section'), 'tensor')
The draws below stay inside these ranges and needn't reach their ends.
Inputs may be any that keep to these rules, and one draw needn't show every extreme that they name: `cache_len`: each prompt has at least 512 live positions; some prompt has exactly 2048.
All inputs are finite; a program needn't handle non-finite values.
Results may differ from the reference program's by a relative error of at most 0.0049.
Values may be sent and summed in bfloat16 or wider, within the bound.
No kernel may reach another device: no remote copies, remote signals or barrier semaphores. Data moves between devices by JAX's collectives and lax.ppermute only.
A program may use at most 64 MiB of HBM per device.

```python
import jax
import jax.numpy as jnp
from jax import lax

D = 8192
HD = 128
KVH = 8
QPK = 8
NEW = 4
CACHE = 2048
TR_DEV = 128
KV = 1024
GROUPS = 128
P_SIZE = 384
TROWS = 16384
N_DP = 64
N_SECTION = 2


def draw_cache_len(key, part):
    own_key = jax.random.fold_in(key, 101)
    base = jax.random.randint(own_key, (P_SIZE,), CACHE // 4, CACHE + 1)
    chosen = jax.random.randint(jax.random.fold_in(own_key, 7), (), 0, P_SIZE)
    return jnp.where(jnp.arange(P_SIZE) == chosen, CACHE, base).astype(jnp.int32)


def draw_query(key, part):
    own_key = jax.random.fold_in(key, 202)
    values = jnp.clip(jax.random.normal(own_key, (P_SIZE, NEW, KVH * QPK * HD), jnp.float32), -4.0, 4.0)
    return values.astype(jnp.bfloat16)


def level_of(key, dims, pieces, least, largest):
    loudness = 1.0
    for axis_at, parts in pieces:
        draws = jax.random.uniform(jax.random.fold_in(jax.random.fold_in(key, 6), axis_at), (parts,), jnp.float32, least / len(pieces), largest / len(pieces))
        loudness = loudness * jnp.repeat(jnp.exp(draws), dims[axis_at] // parts).reshape((-1,) + (1,) * (len(dims) - 1 - axis_at))
    return loudness


def normal_values(key, shape, deviation, bound, split=(), held_as=jnp.bfloat16):
    drawn = deviation * jax.random.normal(key, shape, jnp.float32)
    if split:
        drawn = drawn * level_of(key, shape, split, -0.22, 0.18)
    return jnp.clip(drawn, -bound, bound).astype(held_as)


def setup_inputs(seed: int = 0) -> dict:
    seeds = jax.random.split(jax.random.key(seed), 11)
    return {
        "w_value": normal_values(seeds[0], (D, KV), D ** -0.5, 0.0625, ((0, 128), (1, 8))),
        "hidden_new": normal_values(seeds[1], (P_SIZE, NEW, D), 1.0, 6.0, ((0, 128),)),
        "query": draw_query(jax.random.fold_in(seeds[10], 71), 0),
        "key_new": normal_values(seeds[3], (P_SIZE, NEW, KV), 1.0, 6.0, ((0, 128), (2, 8))),
        "key_cache": normal_values(seeds[4], (P_SIZE, CACHE, KV), 1.0, 6.0, ((0, 128), (2, 8))),
        "value_cache": normal_values(seeds[5], (P_SIZE, CACHE, KV), 1.0, 6.0, ((0, 128), (2, 8))),
        "cache_len": draw_cache_len(jax.random.fold_in(seeds[10], 71), 0),
        "sampled_rows": normal_values(seeds[7], (TROWS, D), 1.0, 6.0, ((0, 128),)),
        "mb_map": jax.vmap(lambda own: jax.random.permutation(own, TR_DEV))(jax.random.split(seeds[8], GROUPS)).reshape((GROUPS, TR_DEV)).astype(jnp.int32),
        "value_target": normal_values(seeds[9], (TROWS, KV), 1.0, 6.0, ((0, 128), (1, 8))),
    }


def attend_prompt(packed):
    query_p, keys_new, keys_cache, values_cache, values_new, length = packed
    scale = 1.0 / jnp.sqrt(jnp.float32(HD))
    query_h = query_p.astype(jnp.float32).reshape(NEW, KVH, QPK, HD)
    kc_heads = keys_cache.astype(jnp.float32).reshape(CACHE, KVH, HD)
    vc_heads = values_cache.astype(jnp.float32).reshape(CACHE, KVH, HD)
    kn_heads = keys_new.astype(jnp.float32).reshape(NEW, KVH, HD)
    vn_heads = values_new.astype(jnp.float32).reshape(NEW, KVH, HD)
    score_cache = jnp.einsum('tgqd,jgd->gtqj', query_h, kc_heads) * scale
    score_new = jnp.einsum('tgqd,ugd->gtqu', query_h, kn_heads) * scale
    live_cache = (jnp.arange(CACHE) < length)[None, None, None, :]
    live_new = (jnp.arange(NEW)[None, :] <= jnp.arange(NEW)[:, None])[None, :, None, :]
    score_cache = jnp.where(live_cache, score_cache, -1e+30)
    score_new = jnp.where(live_new, score_new, -1e+30)
    peak = jnp.maximum(lax.optimization_barrier(jnp.max(score_cache, axis=-1)), lax.optimization_barrier(jnp.max(score_new, axis=-1)))[..., None]
    exp_cache = jnp.where(live_cache, jnp.exp(score_cache - peak), 0.0)
    exp_new = jnp.where(live_new, jnp.exp(score_new - peak), 0.0)
    total = lax.optimization_barrier(jnp.sum(exp_cache, axis=-1, keepdims=True)) + lax.optimization_barrier(jnp.sum(exp_new, axis=-1, keepdims=True))
    prob_cache = (exp_cache / total).astype(jnp.bfloat16).astype(jnp.float32)
    prob_new = (exp_new / total).astype(jnp.bfloat16).astype(jnp.float32)
    result = jnp.einsum('gtqj,jgd->tgqd', prob_cache, vc_heads) + jnp.einsum('gtqu,ugd->tgqd', prob_new, vn_heads)
    return result.reshape(NEW, KVH * QPK * HD).astype(jnp.bfloat16)

def reference(w_value, hidden_new, query, key_new, key_cache, value_cache, cache_len, sampled_rows, mb_map, value_target):
    v_new = jnp.dot(hidden_new.reshape(P_SIZE * NEW, D), w_value, preferred_element_type=jnp.float32)
    v_new = v_new.astype(jnp.bfloat16).reshape(P_SIZE, NEW, KVH * HD)
    attn_out = lax.map(attend_prompt, (query, key_new, key_cache, value_cache, v_new, cache_len))
    groups = N_DP * N_SECTION
    per_peer = TR_DEV // N_DP
    grouped = sampled_rows.reshape(groups, TR_DEV, D)
    ordered = jax.vmap(lambda block, order: block[order])(grouped, mb_map)
    arranged = ordered.reshape(N_DP, N_SECTION, N_DP, per_peer, D).transpose(2, 1, 0, 3, 4)
    train_rows = arranged.reshape(groups * TR_DEV, D)
    v_train = jnp.dot(train_rows, w_value, preferred_element_type=jnp.float32)
    residual_value = (v_train - value_target.astype(jnp.float32)).astype(jnp.bfloat16)
    summed = lax.dot_general(train_rows, residual_value, (((0,), (0,)), ((), ())), preferred_element_type=jnp.float32)
    grad_value = summed / TR_DEV
    return (attn_out, grad_value)
```

```python
import jax
import jax.numpy as jnp
from jax import lax
from jax.sharding import Mesh
from jax.sharding import PartitionSpec as P

HD = 128
QPK = 8
NEW = 4
DP = ("dp_0", "dp_1")
DP_SECTION = ("dp_0", "dp_1", "section")


def per_device(
    w_value,
    hidden_new,
    query,
    key_new,
    key_cache,
    value_cache,
    cache_len,
    sampled_rows,
    mb_map,
    value_target,
):
    replicas = lax.axis_size(DP)
    groups = lax.axis_size(DP_SECTION)
    sections = groups // replicas
    section = lax.axis_index("section")
    row_count, width = sampled_rows.shape
    per_peer = row_count // replicas
    w_rows, width_local = w_value.shape
    order = mb_map[0]
    pieces = value_target.reshape(replicas, 1, per_peer, width_local)
    same = (jnp.arange(sections) == section)[None, :, None, None]
    pieces = jnp.where(same, pieces, jnp.zeros_like(pieces)).reshape(groups, per_peer, width_local)
    outgoing = jnp.concatenate(
        [jnp.broadcast_to(w_value[None], (groups, w_rows, width_local)), pieces], axis=1
    )
    arrived = lax.all_to_all(outgoing, DP_SECTION, 0, 0, tiled=True)
    piece = arrived[:, :w_rows].reshape(width, width_local)
    returned = arrived[:, w_rows:].reshape(replicas, sections, per_peer, width_local)
    returned = jnp.sum(jnp.where(same, returned, jnp.zeros_like(returned)), axis=1)
    returned = returned.reshape(row_count, width_local)
    place = (jnp.arange(row_count)[:, None] == order[None, :]).astype(jnp.bfloat16)
    train_target = jnp.dot(place, returned, preferred_element_type=jnp.float32)
    prompts = hidden_new.shape[0]
    new_rows = hidden_new.reshape(prompts * NEW, hidden_new.shape[2])
    v_new_full = jnp.dot(new_rows, piece, preferred_element_type=jnp.float32)
    v_train = jnp.dot(sampled_rows, piece, preferred_element_type=jnp.float32)
    residual_value = (v_train - train_target).astype(jnp.bfloat16)
    product = lax.dot_general(
        sampled_rows,
        residual_value,
        (((0,), (0,)), ((), ())),
        preferred_element_type=jnp.float32,
    ).astype(jnp.bfloat16)
    terms = lax.all_to_all(
        product.reshape(groups, w_rows, width_local), DP_SECTION, 0, 0, tiled=True
    )
    grad_value = jnp.sum(terms.astype(jnp.float32), axis=0) / row_count
    heads_local = width_local // HD
    cache_size = key_cache.shape[1]
    scale = 1.0 / jnp.sqrt(jnp.float32(HD))
    v_new = v_new_full.astype(jnp.bfloat16).reshape(prompts, NEW, heads_local, HD)
    query_h = query.reshape(prompts, NEW, heads_local, QPK, HD)
    kc_heads = key_cache.reshape(prompts, cache_size, heads_local, HD)
    vc_heads = value_cache.reshape(prompts, cache_size, heads_local, HD)
    kn_heads = key_new.reshape(prompts, NEW, heads_local, HD)
    score_cache = (
        jnp.einsum("ptgqd,pjgd->pgtqj", query_h, kc_heads, preferred_element_type=jnp.float32)
        * scale
    )
    score_new = (
        jnp.einsum("ptgqd,pugd->pgtqu", query_h, kn_heads, preferred_element_type=jnp.float32)
        * scale
    )
    live_cache = (jnp.arange(cache_size)[None, :] < cache_len[:, None])[:, None, None, None, :]
    live_new = (jnp.arange(NEW)[None, :] <= jnp.arange(NEW)[:, None])[None, None, :, None, :]
    score_cache = jnp.where(live_cache, score_cache, -1e30)
    score_new = jnp.where(live_new, score_new, -1e30)
    peak = jnp.maximum(jnp.max(score_cache, axis=-1), jnp.max(score_new, axis=-1))[..., None]
    exp_cache = jnp.where(live_cache, jnp.exp(score_cache - peak), 0.0)
    exp_new = jnp.where(live_new, jnp.exp(score_new - peak), 0.0)
    total = jnp.sum(exp_cache, axis=-1, keepdims=True) + jnp.sum(exp_new, axis=-1, keepdims=True)
    prob_cache = (exp_cache / total).astype(jnp.bfloat16)
    prob_new = (exp_new / total).astype(jnp.bfloat16)
    mixed = jnp.einsum(
        "pgtqj,pjgd->ptgqd", prob_cache, vc_heads, preferred_element_type=jnp.float32
    )
    mixed = mixed + jnp.einsum(
        "pgtqu,pugd->ptgqd", prob_new, v_new, preferred_element_type=jnp.float32
    )
    attn_out = mixed.reshape(prompts, NEW, heads_local * QPK * HD).astype(jnp.bfloat16)
    return (attn_out, grad_value)


def solution(mesh):
    torus = Mesh(
        mesh.devices.reshape(8, 8, mesh.shape["tensor"], mesh.shape["section"]),
        ("dp_0", "dp_1", "tensor", "section"),
    )
    return jax.shard_map(
        per_device,
        mesh=torus,
        in_specs=(
            P(DP_SECTION, "tensor"),
            P(DP_SECTION, None, None),
            P(DP_SECTION, None, "tensor"),
            P(DP_SECTION, None, "tensor"),
            P(DP_SECTION, None, "tensor"),
            P(DP_SECTION, None, "tensor"),
            P(DP_SECTION),
            P(DP_SECTION, None),
            P(DP_SECTION, None),
            P(DP_SECTION, "tensor"),
        ),
        out_specs=(P(DP_SECTION, None, "tensor"), P(DP_SECTION, "tensor")),
        check_vma=False,
    )
```

```python
import jax
import jax.numpy as jnp
from jax import lax
from jax.experimental import pallas as pl
from jax.experimental.pallas import tpu as pltpu
from jax.sharding import Mesh
from jax.sharding import PartitionSpec as P

HD = 128
QPK = 8
NEW = 4
LANES = 128
PAD = 16
DP = ("dp_0", "dp_1")
DP_SECTION = ("dp_0", "dp_1", "section")


def picker(section, w_rows):
    row = lax.broadcasted_iota(jnp.int32, (2 * LANES, LANES), 0)
    col = lax.broadcasted_iota(jnp.int32, (2 * LANES, LANES), 1)
    source = (col // w_rows) * (2 * w_rows) + col % w_rows + section * w_rows
    return (row == source).astype(jnp.float32).astype(jnp.bfloat16)


def halves_body(where_ref, rows_ref, new_ref, keep_ref, send_ref, *, w_rows):
    section, core = where_ref[0], where_ref[1]
    half = rows_ref.shape[0] // 2
    sent_at = pl.ds(pl.multiple_of(core * half, half), half)
    own = picker(section, w_rows)
    other = picker(1 - section, w_rows)
    row_count = rows_ref.shape[0]

    def pick(block, which):
        return jnp.dot(block, which, preferred_element_type=jnp.float32).astype(jnp.bfloat16)

    for tile in range(rows_ref.shape[1] // (2 * LANES)):
        wide = slice(tile * 2 * LANES, (tile + 1) * 2 * LANES)
        thin = slice(tile * LANES, (tile + 1) * LANES)
        keep_ref[:row_count, thin] = pick(rows_ref[:, wide], own)
        keep_ref[row_count:, thin] = pick(new_ref[:, wide], own)
        send_ref[:half, thin] = pick(rows_ref[sent_at, wide], other)
        send_ref[half:, thin] = pick(new_ref[:, wide], other)


def split_halves(where, rows, new_rows, w_rows):
    row_count, width = rows.shape
    steps = 4
    block = width // steps
    kept, sent = row_count + PAD, row_count // 2 + PAD
    return pl.pallas_call(
        lambda *refs: halves_body(*refs, w_rows=w_rows),
        grid=(steps,),
        in_specs=[
            pl.BlockSpec(memory_space=pltpu.SMEM),
            pl.BlockSpec((row_count, block), lambda i: (0, i)),
            pl.BlockSpec((PAD, block), lambda i: (0, i)),
        ],
        out_specs=[
            pl.BlockSpec((kept, block // 2), lambda i: (0, i)),
            pl.BlockSpec((sent, block // 2), lambda i: (0, i)),
        ],
        out_shape=[
            jax.ShapeDtypeStruct((kept, width // 2), jnp.bfloat16),
            jax.ShapeDtypeStruct((sent, width // 2), jnp.bfloat16),
        ],
        cost_estimate=pl.CostEstimate(
            flops=2 * (kept + sent) * width * LANES,
            bytes_accessed=4 * (row_count + PAD) * width,
            transcendentals=0,
        ),
        name="halves",
    )(where, rows, new_rows)


def product_body(kept_ref, first_ref, second_ref, own_ref, res1_ref, res2_ref, out_ref):
    half = res1_ref.shape[0]
    own_rows = own_ref.shape[0]
    contract = (((0,), (0,)), ((), ()))

    def term(rows, residual):
        return lax.dot_general(rows, residual, contract, preferred_element_type=jnp.float32)

    total = term(kept_ref[:own_rows, :], own_ref[...])
    total += term(first_ref[:half, :], res1_ref[...])
    total += term(second_ref[:half, :], res2_ref[...])
    out_ref[...] = total.astype(out_ref.dtype)


def weight_product(kept, first, second, res_own, res1, res2):
    width = kept.shape[1]
    columns = res_own.shape[1]
    steps = 4
    block = width // steps

    def whole(x):
        return pl.BlockSpec(x.shape, lambda i: (0, 0))

    return pl.pallas_call(
        product_body,
        grid=(steps,),
        in_specs=[
            pl.BlockSpec((kept.shape[0], block), lambda i: (0, i)),
            pl.BlockSpec((first.shape[0], block), lambda i: (0, i)),
            pl.BlockSpec((second.shape[0], block), lambda i: (0, i)),
            whole(res_own),
            whole(res1),
            whole(res2),
        ],
        out_specs=pl.BlockSpec((block, columns), lambda i: (i, 0)),
        out_shape=jax.ShapeDtypeStruct((width, columns), jnp.bfloat16),
        cost_estimate=pl.CostEstimate(
            flops=4 * width * columns * res_own.shape[0],
            bytes_accessed=2 * width * (kept.shape[0] + 2 * first.shape[0] + columns),
            transcendentals=0,
        ),
        name="product",
    )(kept, first, second, res_own, res1, res2)


def swap_section(x):
    return lax.ppermute(x, "section", [(0, 1), (1, 0)])


def swap_core(x):
    return lax.ppermute(x, "tensor", [(i, i ^ 1) for i in range(lax.axis_size("tensor"))])


def per_device(
    w_value,
    hidden_new,
    query,
    key_new,
    key_cache,
    value_cache,
    cache_len,
    sampled_rows,
    mb_map,
    value_target,
):
    replicas = lax.axis_size(DP)
    section = lax.axis_index("section")
    core = lax.axis_index("tensor") % 2
    row_count = sampled_rows.shape[0]
    half = row_count // 2
    per_peer = row_count // replicas
    w_rows, width_local = w_value.shape
    order = mb_map[0]
    prompts = hidden_new.shape[0]
    new_count = prompts * NEW
    new_rows = hidden_new.reshape(new_count, hidden_new.shape[2])
    new_rows = jnp.pad(new_rows, ((0, PAD - new_count), (0, 0)))

    where = jnp.stack([section, core]).astype(jnp.int32)
    kept, sent = split_halves(where, sampled_rows, new_rows, w_rows)
    first = swap_section(sent)

    pieces = jnp.pad(value_target.reshape(replicas, per_peer, width_local), ((0, 0), (0, 8 - per_peer), (0, 0)))
    outgoing = jnp.concatenate(
        [jnp.broadcast_to(w_value[None], (replicas, w_rows, width_local)), pieces], axis=1
    )
    arrived = lax.all_to_all(outgoing, DP, 0, 0, tiled=True)
    second = swap_core(first)
    piece = arrived[:, :w_rows].reshape(replicas * w_rows, width_local)
    returned = arrived[:, w_rows : w_rows + per_peer].reshape(row_count, width_local)
    place = (jnp.arange(row_count)[:, None] == order[None, :]).astype(jnp.bfloat16)
    train_target = jnp.dot(place, returned, preferred_element_type=jnp.float32)

    def times(rows):
        return jnp.dot(rows, piece, preferred_element_type=jnp.float32)

    v_kept, v_first, v_second = times(kept), times(first), times(second)
    mine = v_kept[:row_count] - train_target
    upper = core == 1
    theirs = jnp.concatenate(
        [
            jnp.where(upper, v_second[:half], v_first[:half]),
            jnp.where(upper, v_first[:half], v_second[:half]),
        ],
        axis=0,
    )
    partial = jnp.concatenate([mine, theirs, v_first[half:]], axis=0)
    other = swap_section(partial)
    res_own = (mine + other[row_count : 2 * row_count]).astype(jnp.bfloat16)
    res_their = (theirs + other[:row_count]).astype(jnp.bfloat16)
    v_new_rows = (v_kept[row_count:] + other[2 * row_count :])[:new_count]
    res1 = jnp.where(upper, res_their[half:], res_their[:half])
    res2 = jnp.where(upper, res_their[:half], res_their[half:])
    product = weight_product(kept, first, second, res_own, res1, res2)
    terms = lax.all_to_all(
        product.reshape(replicas, w_rows, width_local), DP, 0, 0, tiled=True
    )
    grad_value = jnp.sum(terms.astype(jnp.float32), axis=0) / row_count
    heads_local = width_local // HD
    cache_size = key_cache.shape[1]
    scale = 1.0 / jnp.sqrt(jnp.float32(HD))
    v_new = v_new_rows.astype(jnp.bfloat16).reshape(prompts, NEW, heads_local, HD)
    query_h = query.reshape(prompts, NEW, heads_local, QPK, HD)
    kc_heads = key_cache.reshape(prompts, cache_size, heads_local, HD)
    vc_heads = value_cache.reshape(prompts, cache_size, heads_local, HD)
    kn_heads = key_new.reshape(prompts, NEW, heads_local, HD)
    score_cache = (
        jnp.einsum("ptgqd,pjgd->pgtqj", query_h, kc_heads, preferred_element_type=jnp.float32)
        * scale
    )
    score_new = (
        jnp.einsum("ptgqd,pugd->pgtqu", query_h, kn_heads, preferred_element_type=jnp.float32)
        * scale
    )
    live_cache = (jnp.arange(cache_size)[None, :] < cache_len[:, None])[:, None, None, None, :]
    live_new = (jnp.arange(NEW)[None, :] <= jnp.arange(NEW)[:, None])[None, None, :, None, :]
    score_cache = jnp.where(live_cache, score_cache, -1e30)
    score_new = jnp.where(live_new, score_new, -1e30)
    peak = jnp.maximum(jnp.max(score_cache, axis=-1), jnp.max(score_new, axis=-1))[..., None]
    exp_cache = jnp.where(live_cache, jnp.exp(score_cache - peak), 0.0)
    exp_new = jnp.where(live_new, jnp.exp(score_new - peak), 0.0)
    total = jnp.sum(exp_cache, axis=-1, keepdims=True) + jnp.sum(exp_new, axis=-1, keepdims=True)
    prob_cache = (exp_cache / total).astype(jnp.bfloat16)
    prob_new = (exp_new / total).astype(jnp.bfloat16)
    mixed = jnp.einsum(
        "pgtqj,pjgd->ptgqd", prob_cache, vc_heads, preferred_element_type=jnp.float32
    )
    mixed = mixed + jnp.einsum(
        "pgtqu,pugd->ptgqd", prob_new, v_new, preferred_element_type=jnp.float32
    )
    attn_out = mixed.reshape(prompts, NEW, heads_local * QPK * HD).astype(jnp.bfloat16)
    return (attn_out, grad_value)


def solution(mesh):
    torus = Mesh(
        mesh.devices.reshape(8, 8, mesh.shape["tensor"], mesh.shape["section"]),
        ("dp_0", "dp_1", "tensor", "section"),
    )
    return jax.shard_map(
        per_device,
        mesh=torus,
        in_specs=(
            P(DP_SECTION, "tensor"),
            P(DP_SECTION, None, None),
            P(DP_SECTION, None, "tensor"),
            P(DP_SECTION, None, "tensor"),
            P(DP_SECTION, None, "tensor"),
            P(DP_SECTION, None, "tensor"),
            P(DP_SECTION),
            P(DP_SECTION, None),
            P(DP_SECTION, None),
            P(DP_SECTION, "tensor"),
        ),
        out_specs=(P(DP_SECTION, None, "tensor"), P(DP_SECTION, "tensor")),
        check_vma=False,
    )
```

```python
import jax
import jax.numpy as jnp
from jax import lax
from jax.experimental import pallas as pl
from jax.experimental.pallas import tpu as pltpu
from jax.sharding import Mesh
from jax.sharding import PartitionSpec as P

HD = 128
QPK = 8
NEW = 4
LANES = 128
PAD = 16
SLOT = 8
DP = ("dp_0", "dp_1")
DP_SECTION = ("dp_0", "dp_1", "section")
F32, BF16 = jnp.float32, jnp.bfloat16


def one_hot(cond):
    return cond.astype(F32).astype(BF16)


def picker(section, w_rows):
    row = lax.broadcasted_iota(jnp.int32, (2 * LANES, LANES), 0)
    col = lax.broadcasted_iota(jnp.int32, (2 * LANES, LANES), 1)
    source = (col // w_rows) * (2 * w_rows) + col % w_rows + section * w_rows
    return one_hot(row == source)


def halves_body(where_ref, rows_ref, new_ref, w_ref, target_ref, keep_ref, send_ref, out_ref):
    section, core = where_ref[0], where_ref[1]
    row_count = rows_ref.shape[0]
    half = row_count // 2
    w_rows = w_ref.shape[0]
    sent_at = pl.ds(pl.multiple_of(core * half, half), half)
    own = picker(section, w_rows)
    other = picker(1 - section, w_rows)

    def pick(block, which):
        return jnp.dot(block, which, preferred_element_type=F32).astype(BF16)

    for tile in range(rows_ref.shape[1] // (2 * LANES)):
        wide = slice(tile * 2 * LANES, (tile + 1) * 2 * LANES)
        thin = slice(tile * LANES, (tile + 1) * LANES)
        keep_ref[:row_count, thin] = pick(rows_ref[:, wide], own)
        keep_ref[row_count:, thin] = pick(new_ref[:, wide], own)
        send_ref[:half, thin] = pick(rows_ref[sent_at, wide], other)
        send_ref[half:, thin] = pick(new_ref[:, wide], other)
    peers = out_ref.shape[0]
    targets = target_ref.shape[0]
    per_peer = targets // peers
    row = lax.broadcasted_iota(jnp.int32, (peers * SLOT, targets), 0)
    col = lax.broadcasted_iota(jnp.int32, (peers * SLOT, targets), 1)
    spread = one_hot((row % SLOT < per_peer) & (col == (row // SLOT) * per_peer + row % SLOT))
    slots = jnp.dot(spread, target_ref[...], preferred_element_type=F32)
    slots = slots.reshape(peers, SLOT, -1).astype(BF16)
    for peer in range(peers):
        out_ref[peer, :w_rows, :] = w_ref[...]
        out_ref[peer, w_rows:, :] = slots[peer]


def split_halves(where, rows, new_rows, w_value, target, replicas):
    row_count, width = rows.shape
    w_rows, columns = w_value.shape
    steps = 4
    block = width // steps
    kept, sent = row_count + PAD, row_count // 2 + PAD
    return pl.pallas_call(
        halves_body,
        grid=(steps,),
        in_specs=[
            pl.BlockSpec(memory_space=pltpu.SMEM),
            pl.BlockSpec((row_count, block), lambda i: (0, i)),
            pl.BlockSpec((PAD, block), lambda i: (0, i)),
            pl.BlockSpec((w_rows, columns), lambda i: (0, 0)),
            pl.BlockSpec((row_count // steps, columns), lambda i: (i, 0)),
        ],
        out_specs=[
            pl.BlockSpec((kept, block // 2), lambda i: (0, i)),
            pl.BlockSpec((sent, block // 2), lambda i: (0, i)),
            pl.BlockSpec((replicas // steps, w_rows + SLOT, columns), lambda i: (i, 0, 0)),
        ],
        out_shape=[
            jax.ShapeDtypeStruct((kept, width // 2), BF16),
            jax.ShapeDtypeStruct((sent, width // 2), BF16),
            jax.ShapeDtypeStruct((replicas, w_rows + SLOT, columns), BF16),
        ],
        cost_estimate=pl.CostEstimate(
            flops=2 * (kept + sent) * width * LANES,
            bytes_accessed=4 * (row_count + PAD) * width,
            transcendentals=0,
        ),
        name="halves",
    )(where, rows, new_rows, w_value, target)


def partial_body(
    where_ref, kept_ref, first_ref, second_ref, block_ref, slot_ref, out_ref, new_ref, acc_ref
):
    step, last = pl.program_id(0), pl.num_programs(0) - 1
    core = where_ref[1]
    peers, block_rows, columns = block_ref.shape
    w_rows = block_rows - SLOT
    kept, half = kept_ref.shape[0], first_ref.shape[0] - PAD
    row_count = kept - PAD
    weights = block_ref[:, :w_rows, :].reshape(peers * w_rows, columns)
    slots = block_ref[:, w_rows:, :].reshape(peers * SLOT, columns)
    at = lax.broadcasted_iota(jnp.int32, (row_count, peers * SLOT), 0)
    place = one_hot(at == slot_ref[0])

    def times(rows):
        return jnp.dot(rows, weights, preferred_element_type=F32)

    kept_part = times(kept_ref[...])
    targets = jnp.dot(place, slots, preferred_element_type=F32)
    first_part = times(first_ref[...])
    second_part = times(second_ref[:half, :])
    keep_at, first_at = slice(0, kept), slice(kept, kept + half + PAD)
    second_at = slice(kept + half + PAD, kept + 2 * half + PAD)

    @pl.when(step == 0)
    def _():
        acc_ref[...] = jnp.zeros_like(acc_ref)

    acc_ref[keep_at, :] += kept_part
    acc_ref[:row_count, :] -= targets
    acc_ref[first_at, :] += first_part
    acc_ref[second_at, :] += second_part

    @pl.when(step == last)
    def _():
        out_ref[:row_count, :] = acc_ref[:row_count, :]
        near = pl.ds(pl.multiple_of(row_count + core * half, half), half)
        far = pl.ds(pl.multiple_of(row_count + (1 - core) * half, half), half)
        out_ref[near, :] = acc_ref[kept : kept + half, :]
        out_ref[far, :] = acc_ref[second_at, :]
        out_ref[2 * row_count :, :] = acc_ref[kept + half : kept + half + PAD, :]
        new_ref[...] = acc_ref[row_count:kept, :]


def partial_values(where, kept, first, second, arrived, slot_order):
    replicas, block_rows, columns = arrived.shape
    width = kept.shape[1]
    steps = 4
    block = width // steps
    kept_rows, first_rows = kept.shape[0], first.shape[0]
    row_count = kept_rows - PAD

    def rows_of(x):
        return pl.BlockSpec((x.shape[0], block), lambda i: (0, i))

    return pl.pallas_call(
        partial_body,
        grid=(steps,),
        in_specs=[
            pl.BlockSpec(memory_space=pltpu.SMEM),
            rows_of(kept),
            rows_of(first),
            rows_of(second),
            pl.BlockSpec((replicas // steps, block_rows, columns), lambda i: (i, 0, 0)),
            pl.BlockSpec((1, 1, replicas * SLOT // steps), lambda i: (i, 0, 0)),
        ],
        out_specs=[
            pl.BlockSpec((2 * row_count + PAD, columns), lambda i: (0, 0)),
            pl.BlockSpec((PAD, columns), lambda i: (0, 0)),
        ],
        out_shape=[
            jax.ShapeDtypeStruct((2 * row_count + PAD, columns), F32),
            jax.ShapeDtypeStruct((PAD, columns), F32),
        ],
        scratch_shapes=[pltpu.VMEM((kept_rows + first_rows + first_rows - PAD, columns), F32)],
        cost_estimate=pl.CostEstimate(
            flops=2 * width * columns * (kept_rows + 2 * first_rows),
            bytes_accessed=2 * width * (kept_rows + 2 * first_rows + columns),
            transcendentals=0,
        ),
        name="partial",
    )(where, kept, first, second, arrived, slot_order.reshape(steps, 1, -1))


def turn_body(kept_ref, first_ref, second_ref, out_ref):
    row_count = out_ref.shape[1] // 2
    half = row_count // 2
    out_ref[:, :row_count] = kept_ref[:row_count, :].T
    both = jnp.concatenate([first_ref[:half, :], second_ref[:half, :]], axis=0)
    out_ref[:, row_count:] = both.T


def turned(kept, first, second):
    width = kept.shape[1]
    steps = 4
    block = width // steps
    row_count = kept.shape[0] - PAD

    def rows_of(x):
        return pl.BlockSpec((x.shape[0], block), lambda i: (0, i))

    return pl.pallas_call(
        turn_body,
        grid=(steps,),
        in_specs=[rows_of(kept), rows_of(first), rows_of(second)],
        out_specs=pl.BlockSpec((block, 2 * row_count), lambda i: (i, 0)),
        out_shape=jax.ShapeDtypeStruct((width, 2 * row_count), BF16),
        cost_estimate=pl.CostEstimate(
            flops=0, bytes_accessed=8 * width * row_count, transcendentals=0
        ),
        name="turned",
    )(kept, first, second)


def product_body(where_ref, rows_ref, mine_ref, other_ref, out_ref):
    core = where_ref[1]
    row_count = rows_ref.shape[1] // 2
    half = row_count // 2

    def residual(at, its_at, size):
        return (mine_ref[pl.ds(at, size), :] + other_ref[pl.ds(its_at, size), :]).astype(BF16)

    near = pl.multiple_of(core * half, half)
    far = pl.multiple_of((1 - core) * half, half)
    own = residual(0, row_count, row_count)
    first = residual(row_count + near, near, half)
    second = residual(row_count + far, far, half)
    residuals = jnp.concatenate([own, first, second], axis=0)
    out_ref[...] = jnp.dot(rows_ref[...], residuals, preferred_element_type=F32).astype(BF16)


def weight_product(where, rows, mine, other):
    width, both = rows.shape
    columns = mine.shape[1]
    steps = 4
    block = width // steps
    return pl.pallas_call(
        product_body,
        grid=(steps,),
        in_specs=[
            pl.BlockSpec(memory_space=pltpu.SMEM),
            pl.BlockSpec((block, both), lambda i: (i, 0)),
            pl.BlockSpec(mine.shape, lambda i: (0, 0)),
            pl.BlockSpec(other.shape, lambda i: (0, 0)),
        ],
        out_specs=pl.BlockSpec((block, columns), lambda i: (i, 0)),
        out_shape=jax.ShapeDtypeStruct((width, columns), BF16),
        cost_estimate=pl.CostEstimate(
            flops=2 * width * columns * both,
            bytes_accessed=2 * width * (both + columns),
            transcendentals=0,
        ),
        name="product",
    )(where, rows, mine, other)


def swap_section(x):
    return lax.ppermute(x, "section", [(0, 1), (1, 0)])


def swap_core(x):
    return lax.ppermute(x, "tensor", [(i, i ^ 1) for i in range(lax.axis_size("tensor"))])


def per_device(
    w_value,
    hidden_new,
    query,
    key_new,
    key_cache,
    value_cache,
    cache_len,
    sampled_rows,
    mb_map,
    value_target,
):
    replicas = lax.axis_size(DP)
    section = lax.axis_index("section")
    core = lax.axis_index("tensor") % 2
    row_count = sampled_rows.shape[0]
    per_peer = row_count // replicas
    w_rows, width_local = w_value.shape
    prompts = hidden_new.shape[0]
    new_count = prompts * NEW
    new_rows = hidden_new.reshape(new_count, hidden_new.shape[2])
    new_rows = jnp.pad(new_rows, ((0, PAD - new_count), (0, 0)))
    slot_order = jnp.pad(
        mb_map[0].reshape(replicas, per_peer), ((0, 0), (0, SLOT - per_peer)), constant_values=-1
    )

    where = jnp.stack([section, core]).astype(jnp.int32)
    kept, sent, outgoing = split_halves(
        where, sampled_rows, new_rows, w_value, value_target, replicas
    )
    first = swap_section(sent)
    arrived = lax.all_to_all(outgoing, DP, 0, 0, tiled=True)
    second = swap_core(first)
    partial, new_part = partial_values(where, kept, first, second, arrived, slot_order)
    other = swap_section(partial)
    rows_turned = turned(kept, first, second)
    v_new_rows = (new_part + other[2 * row_count :])[:new_count]
    product = weight_product(where, rows_turned, partial, other)
    terms = lax.all_to_all(
        product.reshape(replicas, w_rows, width_local), DP, 0, 0, tiled=True
    )
    grad_value = jnp.sum(terms.astype(jnp.float32), axis=0) / row_count
    heads_local = width_local // HD
    cache_size = key_cache.shape[1]
    scale = 1.0 / jnp.sqrt(jnp.float32(HD))
    v_new = v_new_rows.astype(jnp.bfloat16).reshape(prompts, NEW, heads_local, HD)
    query_h = query.reshape(prompts, NEW, heads_local, QPK, HD)
    kc_heads = key_cache.reshape(prompts, cache_size, heads_local, HD)
    vc_heads = value_cache.reshape(prompts, cache_size, heads_local, HD)
    kn_heads = key_new.reshape(prompts, NEW, heads_local, HD)
    score_cache = (
        jnp.einsum("ptgqd,pjgd->pgtqj", query_h, kc_heads, preferred_element_type=jnp.float32)
        * scale
    )
    score_new = (
        jnp.einsum("ptgqd,pugd->pgtqu", query_h, kn_heads, preferred_element_type=jnp.float32)
        * scale
    )
    live_cache = (jnp.arange(cache_size)[None, :] < cache_len[:, None])[:, None, None, None, :]
    live_new = (jnp.arange(NEW)[None, :] <= jnp.arange(NEW)[:, None])[None, None, :, None, :]
    score_cache = jnp.where(live_cache, score_cache, -1e30)
    score_new = jnp.where(live_new, score_new, -1e30)
    peak = jnp.maximum(jnp.max(score_cache, axis=-1), jnp.max(score_new, axis=-1))[..., None]
    exp_cache = jnp.where(live_cache, jnp.exp(score_cache - peak), 0.0)
    exp_new = jnp.where(live_new, jnp.exp(score_new - peak), 0.0)
    total = jnp.sum(exp_cache, axis=-1, keepdims=True) + jnp.sum(exp_new, axis=-1, keepdims=True)
    prob_cache = (exp_cache / total).astype(jnp.bfloat16)
    prob_new = (exp_new / total).astype(jnp.bfloat16)
    mixed = jnp.einsum(
        "pgtqj,pjgd->ptgqd", prob_cache, vc_heads, preferred_element_type=jnp.float32
    )
    mixed = mixed + jnp.einsum(
        "pgtqu,pugd->ptgqd", prob_new, v_new, preferred_element_type=jnp.float32
    )
    attn_out = mixed.reshape(prompts, NEW, heads_local * QPK * HD).astype(jnp.bfloat16)
    return (attn_out, grad_value)


def solution(mesh):
    torus = Mesh(
        mesh.devices.reshape(8, 8, mesh.shape["tensor"], mesh.shape["section"]),
        ("dp_0", "dp_1", "tensor", "section"),
    )
    return jax.shard_map(
        per_device,
        mesh=torus,
        in_specs=(
            P(DP_SECTION, "tensor"),
            P(DP_SECTION, None, None),
            P(DP_SECTION, None, "tensor"),
            P(DP_SECTION, None, "tensor"),
            P(DP_SECTION, None, "tensor"),
            P(DP_SECTION, None, "tensor"),
            P(DP_SECTION),
            P(DP_SECTION, None),
            P(DP_SECTION, None),
            P(DP_SECTION, "tensor"),
        ),
        out_specs=(P(DP_SECTION, None, "tensor"), P(DP_SECTION, "tensor")),
        check_vma=False,
    )
```

```python
import jax
import jax.numpy as jnp
from jax import lax
from jax.experimental import pallas as pl
from jax.experimental.pallas import tpu as pltpu
from jax.sharding import Mesh
from jax.sharding import PartitionSpec as P

HD = 128
QPK = 8
NEW = 4
LANES = 128
PAD = 16
SLOT = 8
GRANT = 20 * 1024 * 1024
DP = ("dp_0", "dp_1")
DP_SECTION = ("dp_0", "dp_1", "section")
F32, BF16 = jnp.float32, jnp.bfloat16


def one_hot(cond):
    return cond.astype(F32).astype(BF16)


def picker(section, w_rows):
    row = lax.broadcasted_iota(jnp.int32, (2 * LANES, LANES), 0)
    col = lax.broadcasted_iota(jnp.int32, (2 * LANES, LANES), 1)
    source = (col // w_rows) * (2 * w_rows) + col % w_rows + section * w_rows
    return one_hot(row == source)


def core_index():
    return lax.axis_index("tensor") % 2


def halves_body(rows_ref, new_ref, w_ref, target_ref, keep_ref, send_ref, out_ref, new_scr):
    section, core = lax.axis_index("section"), core_index()
    row_count = rows_ref.shape[0]
    half = row_count // 2
    w_rows = w_ref.shape[0]
    sent_at = pl.ds(pl.multiple_of(core * half, half), half)
    own = picker(section, w_rows)
    other = picker(1 - section, w_rows)

    prompts, new, _ = new_ref.shape
    new_scr[...] = jnp.zeros_like(new_scr)
    for prompt in range(prompts):
        new_scr[prompt * new : (prompt + 1) * new, :] = new_ref[prompt].astype(F32)

    def pick(block, which):
        return jnp.dot(block, which, preferred_element_type=F32).astype(BF16)

    for tile in range(rows_ref.shape[1] // (2 * LANES)):
        wide = slice(tile * 2 * LANES, (tile + 1) * 2 * LANES)
        thin = slice(tile * LANES, (tile + 1) * LANES)
        keep_ref[:row_count, thin] = pick(rows_ref[:, wide], own)
        fresh = new_scr[:, wide].astype(BF16)
        keep_ref[row_count:, thin] = pick(fresh, own)
        send_ref[:half, thin] = pick(rows_ref[sent_at, wide], other)
        send_ref[half:, thin] = pick(fresh, other)
    peers = out_ref.shape[0]
    targets = target_ref.shape[0]
    per_peer = targets // peers
    row = lax.broadcasted_iota(jnp.int32, (peers * SLOT, targets), 0)
    col = lax.broadcasted_iota(jnp.int32, (peers * SLOT, targets), 1)
    spread = one_hot((row % SLOT < per_peer) & (col == (row // SLOT) * per_peer + row % SLOT))
    slots = jnp.dot(spread, target_ref[...], preferred_element_type=F32)
    slots = slots.reshape(peers, SLOT, -1).astype(BF16)
    for peer in range(peers):
        out_ref[peer, :w_rows, :] = w_ref[...]
        out_ref[peer, w_rows:, :] = slots[peer]


def split_halves(rows, new_rows, w_value, target, replicas):
    row_count, width = rows.shape
    w_rows, columns = w_value.shape
    steps = 4
    block = width // steps
    kept, sent = row_count + PAD, row_count // 2 + PAD
    return pl.pallas_call(
        halves_body,
        grid=(steps,),
        in_specs=[
            pl.BlockSpec((row_count, block), lambda i: (0, i)),
            pl.BlockSpec((*new_rows.shape[:2], block), lambda i: (0, 0, i)),
            pl.BlockSpec((w_rows, columns), lambda i: (0, 0)),
            pl.BlockSpec((row_count // steps, columns), lambda i: (i, 0)),
        ],
        out_specs=[
            pl.BlockSpec((kept, block // 2), lambda i: (0, i)),
            pl.BlockSpec((sent, block // 2), lambda i: (0, i)),
            pl.BlockSpec((replicas // steps, w_rows + SLOT, columns), lambda i: (i, 0, 0)),
        ],
        out_shape=[
            jax.ShapeDtypeStruct((kept, width // 2), BF16),
            jax.ShapeDtypeStruct((sent, width // 2), BF16),
            jax.ShapeDtypeStruct((replicas, w_rows + SLOT, columns), BF16),
        ],
        cost_estimate=pl.CostEstimate(
            flops=2 * (kept + sent) * width * LANES,
            bytes_accessed=4 * (row_count + PAD) * width,
            transcendentals=0,
        ),
        scratch_shapes=[pltpu.VMEM((PAD, block), F32)],
        name="halves",
    )(rows, new_rows, w_value, target)


VMEM = pl.BlockSpec(memory_space=pltpu.VMEM)


def partial_body(
    kept_ref, first_ref, second_ref, block_ref, slot_ref, out_ref, new_ref
):
    core = core_index()
    peers, block_rows, columns = block_ref.shape
    w_rows = block_rows - SLOT
    kept, half = kept_ref.shape[0], first_ref.shape[0] - PAD
    row_count = kept - PAD
    weights = block_ref[:, :w_rows, :].reshape(peers * w_rows, columns)
    slots = block_ref[:, w_rows:, :].reshape(peers * SLOT, columns)
    at = lax.broadcasted_iota(jnp.int32, (row_count, peers * SLOT), 0)
    place = one_hot(at == slot_ref[...])
    targets = jnp.dot(place, slots, preferred_element_type=F32)

    def times(rows):
        return jnp.dot(rows, weights, preferred_element_type=F32)

    kept_part = times(kept_ref[...])
    first_part = times(first_ref[...])
    second_part = times(second_ref[:half, :])
    near = pl.ds(pl.multiple_of(row_count + core * half, half), half)
    far = pl.ds(pl.multiple_of(row_count + (1 - core) * half, half), half)
    out_ref[:row_count, :] = kept_part[:row_count] - targets
    out_ref[near, :] = first_part[:half]
    out_ref[far, :] = second_part
    out_ref[2 * row_count :, :] = first_part[half:]
    new_ref[...] = kept_part[row_count:]


def partial_values(kept, first, second, arrived, slot_order):
    columns = arrived.shape[2]
    width = kept.shape[1]
    row_count = kept.shape[0] - PAD
    rows = kept.shape[0] + 2 * first.shape[0]
    return pl.pallas_call(
        partial_body,
        in_specs=[VMEM] * 5,
        out_specs=[VMEM, VMEM],
        out_shape=[
            jax.ShapeDtypeStruct((2 * row_count + PAD, columns), F32),
            jax.ShapeDtypeStruct((PAD, columns), F32),
        ],
        cost_estimate=pl.CostEstimate(
            flops=2 * width * columns * rows,
            bytes_accessed=2 * width * (rows + columns),
            transcendentals=0,
        ),
        compiler_params=pltpu.CompilerParams(vmem_limit_bytes=GRANT),
        name="partial",
    )(kept, first, second, arrived, slot_order.reshape(1, -1))


def turn_body(kept_ref, first_ref, second_ref, out_ref):
    width, both = out_ref.shape
    row_count = both // 2
    half = row_count // 2
    block = 512
    for start in range(0, width, block):
        at = slice(start, start + block)
        out_ref[at, :row_count] = kept_ref[:row_count, at].T
        pair = jnp.concatenate([first_ref[:half, at], second_ref[:half, at]], axis=0)
        out_ref[at, row_count:] = pair.T


def turned(kept, first, second):
    width = kept.shape[1]
    row_count = kept.shape[0] - PAD
    return pl.pallas_call(
        turn_body,
        in_specs=[VMEM, VMEM, VMEM],
        out_specs=VMEM,
        out_shape=jax.ShapeDtypeStruct((width, 2 * row_count), BF16),
        cost_estimate=pl.CostEstimate(
            flops=0, bytes_accessed=8 * width * row_count, transcendentals=0
        ),
        compiler_params=pltpu.CompilerParams(vmem_limit_bytes=GRANT),
        name="turned",
    )(kept, first, second)


def product_body(rows_ref, mine_ref, other_ref, out_ref):
    core = core_index()
    row_count = rows_ref.shape[1] // 2
    half = row_count // 2

    def residual(at, its_at, size):
        return (mine_ref[pl.ds(at, size), :] + other_ref[pl.ds(its_at, size), :]).astype(BF16)

    near = pl.multiple_of(core * half, half)
    far = pl.multiple_of((1 - core) * half, half)
    own = residual(0, row_count, row_count)
    first = residual(row_count + near, near, half)
    second = residual(row_count + far, far, half)
    residuals = jnp.concatenate([own, first, second], axis=0)
    out_ref[...] = jnp.dot(rows_ref[...], residuals, preferred_element_type=F32).astype(BF16)


def weight_product(rows, mine, other):
    width, both = rows.shape
    columns = mine.shape[1]
    return pl.pallas_call(
        product_body,
        in_specs=[VMEM] * 3,
        out_specs=VMEM,
        out_shape=jax.ShapeDtypeStruct((width, columns), BF16),
        cost_estimate=pl.CostEstimate(
            flops=2 * width * columns * both,
            bytes_accessed=2 * width * (both + columns),
            transcendentals=0,
        ),
        compiler_params=pltpu.CompilerParams(vmem_limit_bytes=GRANT),
        name="product",
    )(rows, mine, other)


def swap_section(x):
    return lax.ppermute(x, "section", [(0, 1), (1, 0)])


def swap_core(x):
    return lax.ppermute(x, "tensor", [(i, i ^ 1) for i in range(lax.axis_size("tensor"))])


def per_device(
    w_value,
    hidden_new,
    query,
    key_new,
    key_cache,
    value_cache,
    cache_len,
    sampled_rows,
    mb_map,
    value_target,
):
    replicas = lax.axis_size(DP)
    row_count = sampled_rows.shape[0]
    per_peer = row_count // replicas
    w_rows, width_local = w_value.shape
    prompts = hidden_new.shape[0]
    new_count = prompts * NEW
    slot_order = jnp.pad(
        mb_map[0].reshape(replicas, per_peer), ((0, 0), (0, SLOT - per_peer)), constant_values=-1
    )

    kept, sent, outgoing = split_halves(
        sampled_rows, hidden_new, w_value, value_target, replicas
    )
    first = swap_section(sent)
    arrived = lax.all_to_all(outgoing, DP, 0, 0, tiled=True)
    second = swap_core(first)
    partial, new_part = partial_values(kept, first, second, arrived, slot_order)
    other = swap_section(partial)
    rows_turned = turned(kept, first, second)
    v_new_rows = (new_part + other[2 * row_count :])[:new_count]
    product = weight_product(rows_turned, partial, other)
    terms = lax.all_to_all(
        product.reshape(replicas, w_rows, width_local), DP, 0, 0, tiled=True
    )
    grad_value = jnp.sum(terms.astype(jnp.float32), axis=0) / row_count
    heads_local = width_local // HD
    cache_size = key_cache.shape[1]
    scale = 1.0 / jnp.sqrt(jnp.float32(HD))
    v_new = v_new_rows.astype(jnp.bfloat16).reshape(prompts, NEW, heads_local, HD)
    query_h = query.reshape(prompts, NEW, heads_local, QPK, HD)
    kc_heads = key_cache.reshape(prompts, cache_size, heads_local, HD)
    vc_heads = value_cache.reshape(prompts, cache_size, heads_local, HD)
    kn_heads = key_new.reshape(prompts, NEW, heads_local, HD)
    score_cache = (
        jnp.einsum("ptgqd,pjgd->pgtqj", query_h, kc_heads, preferred_element_type=jnp.float32)
        * scale
    )
    score_new = (
        jnp.einsum("ptgqd,pugd->pgtqu", query_h, kn_heads, preferred_element_type=jnp.float32)
        * scale
    )
    live_cache = (jnp.arange(cache_size)[None, :] < cache_len[:, None])[:, None, None, None, :]
    live_new = (jnp.arange(NEW)[None, :] <= jnp.arange(NEW)[:, None])[None, None, :, None, :]
    score_cache = jnp.where(live_cache, score_cache, -1e30)
    score_new = jnp.where(live_new, score_new, -1e30)
    peak = jnp.maximum(jnp.max(score_cache, axis=-1), jnp.max(score_new, axis=-1))[..., None]
    exp_cache = jnp.where(live_cache, jnp.exp(score_cache - peak), 0.0)
    exp_new = jnp.where(live_new, jnp.exp(score_new - peak), 0.0)
    total = jnp.sum(exp_cache, axis=-1, keepdims=True) + jnp.sum(exp_new, axis=-1, keepdims=True)
    prob_cache = (exp_cache / total).astype(jnp.bfloat16)
    prob_new = (exp_new / total).astype(jnp.bfloat16)
    mixed = jnp.einsum(
        "pgtqj,pjgd->ptgqd", prob_cache, vc_heads, preferred_element_type=jnp.float32
    )
    mixed = mixed + jnp.einsum(
        "pgtqu,pugd->ptgqd", prob_new, v_new, preferred_element_type=jnp.float32
    )
    attn_out = mixed.reshape(prompts, NEW, heads_local * QPK * HD).astype(jnp.bfloat16)
    return (attn_out, grad_value)


def solution(mesh):
    torus = Mesh(
        mesh.devices.reshape(8, 8, mesh.shape["tensor"], mesh.shape["section"]),
        ("dp_0", "dp_1", "tensor", "section"),
    )
    return jax.shard_map(
        per_device,
        mesh=torus,
        in_specs=(
            P(DP_SECTION, "tensor"),
            P(DP_SECTION, None, None),
            P(DP_SECTION, None, "tensor"),
            P(DP_SECTION, None, "tensor"),
            P(DP_SECTION, None, "tensor"),
            P(DP_SECTION, None, "tensor"),
            P(DP_SECTION),
            P(DP_SECTION, None),
            P(DP_SECTION, None),
            P(DP_SECTION, "tensor"),
        ),
        out_specs=(P(DP_SECTION, None, "tensor"), P(DP_SECTION, "tensor")),
        check_vma=False,
    )
```

```python
import jax
import jax.numpy as jnp
from jax import lax
from jax.experimental import pallas as pl
from jax.experimental.pallas import tpu as pltpu
from jax.sharding import Mesh
from jax.sharding import PartitionSpec as P

HD = 128
QPK = 8
NEW = 4
LANES = 128
PAD = 16
SLOT = 8
GRANT = 20 * 1024 * 1024
DP = ("dp_0", "dp_1")
DP_SECTION = ("dp_0", "dp_1", "section")
F32, BF16 = jnp.float32, jnp.bfloat16


def one_hot(cond):
    return cond.astype(F32).astype(BF16)


def picker(section, w_rows):
    row = lax.broadcasted_iota(jnp.int32, (2 * LANES, LANES), 0)
    col = lax.broadcasted_iota(jnp.int32, (2 * LANES, LANES), 1)
    source = (col // w_rows) * (2 * w_rows) + col % w_rows + section * w_rows
    return one_hot(row == source)


def core_index():
    return lax.axis_index("tensor") % 2


def pick(block, which):
    return jnp.dot(block, which, preferred_element_type=F32).astype(BF16)


def fresh_rows(new_ref, new_scr):
    prompts, new, _ = new_ref.shape
    new_scr[...] = jnp.zeros_like(new_scr)
    for prompt in range(prompts):
        new_scr[prompt * new : (prompt + 1) * new, :] = new_ref[prompt].astype(F32)


def tiles(width):
    for tile in range(width // (2 * LANES)):
        wide = slice(tile * 2 * LANES, (tile + 1) * 2 * LANES)
        thin = slice(tile * LANES, (tile + 1) * LANES)
        yield wide, thin


def sent_body(rows_ref, new_ref, w_ref, target_ref, send_ref, out_ref, new_scr):
    half = rows_ref.shape[0]
    w_rows = w_ref.shape[0]
    other = picker(1 - lax.axis_index("section"), w_rows)
    fresh_rows(new_ref, new_scr)
    for wide, thin in tiles(rows_ref.shape[1]):
        send_ref[:half, thin] = pick(rows_ref[:, wide], other)
        send_ref[half:, thin] = pick(new_scr[:, wide].astype(BF16), other)
    peers = out_ref.shape[0]
    targets = target_ref.shape[0]
    per_peer = targets // peers
    row = lax.broadcasted_iota(jnp.int32, (peers * SLOT, targets), 0)
    col = lax.broadcasted_iota(jnp.int32, (peers * SLOT, targets), 1)
    spread = one_hot((row % SLOT < per_peer) & (col == (row // SLOT) * per_peer + row % SLOT))
    slots = jnp.dot(spread, target_ref[...], preferred_element_type=F32)
    slots = slots.reshape(peers, SLOT, -1).astype(BF16)
    for peer in range(peers):
        out_ref[peer, :w_rows, :] = w_ref[...]
        out_ref[peer, w_rows:, :] = slots[peer]


def sent_half(rows, new_rows, w_value, target, replicas):
    row_count, width = rows.shape
    w_rows, columns = w_value.shape
    half = row_count // 2
    steps = 4
    block = width // steps
    sent = half + PAD
    return pl.pallas_call(
        sent_body,
        grid=(steps,),
        in_specs=[
            pl.BlockSpec((half, block), lambda i: (core_index(), i)),
            pl.BlockSpec((*new_rows.shape[:2], block), lambda i: (0, 0, i)),
            pl.BlockSpec((w_rows, columns), lambda i: (0, 0)),
            pl.BlockSpec((row_count // steps, columns), lambda i: (i, 0)),
        ],
        out_specs=[
            pl.BlockSpec((sent, block // 2), lambda i: (0, i)),
            pl.BlockSpec((replicas // steps, w_rows + SLOT, columns), lambda i: (i, 0, 0)),
        ],
        out_shape=[
            jax.ShapeDtypeStruct((sent, width // 2), BF16),
            jax.ShapeDtypeStruct((replicas, w_rows + SLOT, columns), BF16),
        ],
        cost_estimate=pl.CostEstimate(
            flops=2 * sent * width * LANES,
            bytes_accessed=4 * sent * width,
            transcendentals=0,
        ),
        scratch_shapes=[pltpu.VMEM((PAD, block), F32)],
        name="sent",
    )(rows, new_rows, w_value, target)


def kept_body(rows_ref, new_ref, keep_ref, new_scr, *, w_rows):
    row_count = rows_ref.shape[0]
    own = picker(lax.axis_index("section"), w_rows)
    fresh_rows(new_ref, new_scr)
    for wide, thin in tiles(rows_ref.shape[1]):
        keep_ref[:row_count, thin] = pick(rows_ref[:, wide], own)
        keep_ref[row_count:, thin] = pick(new_scr[:, wide].astype(BF16), own)


def kept_half(rows, new_rows, w_rows):
    row_count, width = rows.shape
    steps = 4
    block = width // steps
    kept = row_count + PAD
    return pl.pallas_call(
        lambda *refs: kept_body(*refs, w_rows=w_rows),
        grid=(steps,),
        in_specs=[
            pl.BlockSpec((row_count, block), lambda i: (0, i)),
            pl.BlockSpec((*new_rows.shape[:2], block), lambda i: (0, 0, i)),
        ],
        out_specs=pl.BlockSpec((kept, block // 2), lambda i: (0, i)),
        out_shape=jax.ShapeDtypeStruct((kept, width // 2), BF16),
        cost_estimate=pl.CostEstimate(
            flops=2 * kept * width * LANES,
            bytes_accessed=4 * kept * width,
            transcendentals=0,
        ),
        scratch_shapes=[pltpu.VMEM((PAD, block), F32)],
        compiler_params=pltpu.CompilerParams(vmem_limit_bytes=GRANT),
        name="kept",
    )(rows, new_rows)


VMEM = pl.BlockSpec(memory_space=pltpu.VMEM)


def partial_body(
    kept_ref, first_ref, second_ref, block_ref, slot_ref, out_ref, new_ref
):
    core = core_index()
    peers, block_rows, columns = block_ref.shape
    w_rows = block_rows - SLOT
    kept, half = kept_ref.shape[0], first_ref.shape[0] - PAD
    row_count = kept - PAD
    weights = block_ref[:, :w_rows, :].reshape(peers * w_rows, columns)
    slots = block_ref[:, w_rows:, :].reshape(peers * SLOT, columns)
    at = lax.broadcasted_iota(jnp.int32, (row_count, peers * SLOT), 0)
    place = one_hot(at == slot_ref[...])
    targets = jnp.dot(place, slots, preferred_element_type=F32)

    def times(rows):
        return jnp.dot(rows, weights, preferred_element_type=F32)

    kept_part = times(kept_ref[...])
    first_part = times(first_ref[...])
    second_part = times(second_ref[:half, :])
    near = pl.ds(pl.multiple_of(row_count + core * half, half), half)
    far = pl.ds(pl.multiple_of(row_count + (1 - core) * half, half), half)
    out_ref[:row_count, :] = kept_part[:row_count] - targets
    out_ref[near, :] = first_part[:half]
    out_ref[far, :] = second_part
    out_ref[2 * row_count :, :] = first_part[half:]
    new_ref[...] = kept_part[row_count:]


def partial_values(kept, first, second, arrived, slot_order):
    columns = arrived.shape[2]
    width = kept.shape[1]
    row_count = kept.shape[0] - PAD
    rows = kept.shape[0] + 2 * first.shape[0]
    return pl.pallas_call(
        partial_body,
        in_specs=[VMEM] * 5,
        out_specs=[VMEM, VMEM],
        out_shape=[
            jax.ShapeDtypeStruct((2 * row_count + PAD, columns), F32),
            jax.ShapeDtypeStruct((PAD, columns), F32),
        ],
        cost_estimate=pl.CostEstimate(
            flops=2 * width * columns * rows,
            bytes_accessed=2 * width * (rows + columns),
            transcendentals=0,
        ),
        compiler_params=pltpu.CompilerParams(vmem_limit_bytes=GRANT),
        name="partial",
    )(kept, first, second, arrived, slot_order.reshape(1, -1))


def turn_body(kept_ref, first_ref, second_ref, out_ref):
    width, both = out_ref.shape
    row_count = both // 2
    half = row_count // 2
    block = 512
    for start in range(0, width, block):
        at = slice(start, start + block)
        out_ref[at, :row_count] = kept_ref[:row_count, at].T
        pair = jnp.concatenate([first_ref[:half, at], second_ref[:half, at]], axis=0)
        out_ref[at, row_count:] = pair.T


def turned(kept, first, second):
    width = kept.shape[1]
    row_count = kept.shape[0] - PAD
    return pl.pallas_call(
        turn_body,
        in_specs=[VMEM, VMEM, VMEM],
        out_specs=VMEM,
        out_shape=jax.ShapeDtypeStruct((width, 2 * row_count), BF16),
        cost_estimate=pl.CostEstimate(
            flops=0, bytes_accessed=8 * width * row_count, transcendentals=0
        ),
        compiler_params=pltpu.CompilerParams(vmem_limit_bytes=GRANT),
        name="turned",
    )(kept, first, second)


def product_body(rows_ref, mine_ref, other_ref, out_ref):
    core = core_index()
    row_count = rows_ref.shape[1] // 2
    half = row_count // 2

    def residual(at, its_at, size):
        return (mine_ref[pl.ds(at, size), :] + other_ref[pl.ds(its_at, size), :]).astype(BF16)

    near = pl.multiple_of(core * half, half)
    far = pl.multiple_of((1 - core) * half, half)
    own = residual(0, row_count, row_count)
    first = residual(row_count + near, near, half)
    second = residual(row_count + far, far, half)
    residuals = jnp.concatenate([own, first, second], axis=0)
    out_ref[...] = jnp.dot(rows_ref[...], residuals, preferred_element_type=F32).astype(BF16)


def weight_product(rows, mine, other):
    width, both = rows.shape
    columns = mine.shape[1]
    return pl.pallas_call(
        product_body,
        in_specs=[VMEM] * 3,
        out_specs=VMEM,
        out_shape=jax.ShapeDtypeStruct((width, columns), BF16),
        cost_estimate=pl.CostEstimate(
            flops=2 * width * columns * both,
            bytes_accessed=2 * width * (both + columns),
            transcendentals=0,
        ),
        compiler_params=pltpu.CompilerParams(vmem_limit_bytes=GRANT),
        name="product",
    )(rows, mine, other)


def swap_section(x):
    return lax.ppermute(x, "section", [(0, 1), (1, 0)])


def swap_core(x):
    return lax.ppermute(x, "tensor", [(i, i ^ 1) for i in range(lax.axis_size("tensor"))])


def per_device(
    w_value,
    hidden_new,
    query,
    key_new,
    key_cache,
    value_cache,
    cache_len,
    sampled_rows,
    mb_map,
    value_target,
):
    replicas = lax.axis_size(DP)
    row_count = sampled_rows.shape[0]
    per_peer = row_count // replicas
    w_rows, width_local = w_value.shape
    prompts = hidden_new.shape[0]
    new_count = prompts * NEW
    slot_order = jnp.pad(
        mb_map[0].reshape(replicas, per_peer), ((0, 0), (0, SLOT - per_peer)), constant_values=-1
    )

    sent, outgoing = sent_half(sampled_rows, hidden_new, w_value, value_target, replicas)
    kept = kept_half(sampled_rows, hidden_new, w_rows)
    first = swap_section(sent)
    arrived = lax.all_to_all(outgoing, DP, 0, 0, tiled=True)
    second = swap_core(first)
    partial, new_part = partial_values(kept, first, second, arrived, slot_order)
    other = swap_section(partial)
    rows_turned = turned(kept, first, second)
    v_new_rows = (new_part + other[2 * row_count :])[:new_count]
    product = weight_product(rows_turned, partial, other)
    terms = lax.all_to_all(
        product.reshape(replicas, w_rows, width_local), DP, 0, 0, tiled=True
    )
    grad_value = jnp.sum(terms.astype(jnp.float32) * (1.0 / row_count), axis=0)
    heads_local = width_local // HD
    cache_size = key_cache.shape[1]
    scale = 1.0 / jnp.sqrt(jnp.float32(HD))
    v_new = v_new_rows.astype(jnp.bfloat16).reshape(prompts, NEW, heads_local, HD)
    query_h = query.reshape(prompts, NEW, heads_local, QPK, HD)
    kc_heads = key_cache.reshape(prompts, cache_size, heads_local, HD)
    vc_heads = value_cache.reshape(prompts, cache_size, heads_local, HD)
    kn_heads = key_new.reshape(prompts, NEW, heads_local, HD)
    score_cache = (
        jnp.einsum("ptgqd,pjgd->pgtqj", query_h, kc_heads, preferred_element_type=jnp.float32)
        * scale
    )
    score_new = (
        jnp.einsum("ptgqd,pugd->pgtqu", query_h, kn_heads, preferred_element_type=jnp.float32)
        * scale
    )
    live_cache = (jnp.arange(cache_size)[None, :] < cache_len[:, None])[:, None, None, None, :]
    live_new = (jnp.arange(NEW)[None, :] <= jnp.arange(NEW)[:, None])[None, None, :, None, :]
    score_cache = jnp.where(live_cache, score_cache, -1e30)
    score_new = jnp.where(live_new, score_new, -1e30)
    peak = jnp.maximum(jnp.max(score_cache, axis=-1), jnp.max(score_new, axis=-1))[..., None]
    exp_cache = jnp.where(live_cache, jnp.exp(score_cache - peak), 0.0)
    exp_new = jnp.where(live_new, jnp.exp(score_new - peak), 0.0)
    total = jnp.sum(exp_cache, axis=-1, keepdims=True) + jnp.sum(exp_new, axis=-1, keepdims=True)
    prob_cache = (exp_cache / total).astype(jnp.bfloat16)
    prob_new = (exp_new / total).astype(jnp.bfloat16)
    mixed = jnp.einsum(
        "pgtqj,pjgd->ptgqd", prob_cache, vc_heads, preferred_element_type=jnp.float32
    )
    mixed = mixed + jnp.einsum(
        "pgtqu,pugd->ptgqd", prob_new, v_new, preferred_element_type=jnp.float32
    )
    attn_out = mixed.reshape(prompts, NEW, heads_local * QPK * HD).astype(jnp.bfloat16)
    return (attn_out, grad_value)


def solution(mesh):
    torus = Mesh(
        mesh.devices.reshape(8, 8, mesh.shape["tensor"], mesh.shape["section"]),
        ("dp_0", "dp_1", "tensor", "section"),
    )
    return jax.shard_map(
        per_device,
        mesh=torus,
        in_specs=(
            P(DP_SECTION, "tensor"),
            P(DP_SECTION, None, None),
            P(DP_SECTION, None, "tensor"),
            P(DP_SECTION, None, "tensor"),
            P(DP_SECTION, None, "tensor"),
            P(DP_SECTION, None, "tensor"),
            P(DP_SECTION),
            P(DP_SECTION, None),
            P(DP_SECTION, None),
            P(DP_SECTION, "tensor"),
        ),
        out_specs=(P(DP_SECTION, None, "tensor"), P(DP_SECTION, "tensor")),
        check_vma=False,
    )
```

```python
import jax
import jax.numpy as jnp
from jax import lax
from jax.experimental import pallas as pl
from jax.experimental.pallas import tpu as pltpu
from jax.sharding import Mesh
from jax.sharding import PartitionSpec as P

HD = 128
QPK = 8
NEW = 4
LANES = 128
PAD = 16
SLOT = 8
GRANT = 20 * 1024 * 1024
DP = ("dp_0", "dp_1")
DP_SECTION = ("dp_0", "dp_1", "section")
F32, BF16 = jnp.float32, jnp.bfloat16


def one_hot(cond):
    return cond.astype(F32).astype(BF16)


def picker(section, w_rows):
    row = lax.broadcasted_iota(jnp.int32, (2 * LANES, LANES), 0)
    col = lax.broadcasted_iota(jnp.int32, (2 * LANES, LANES), 1)
    source = (col // w_rows) * (2 * w_rows) + col % w_rows + section * w_rows
    return one_hot(row == source)


def core_index():
    return lax.axis_index("tensor") % 2


def pick(block, which):
    return jnp.dot(block, which, preferred_element_type=F32).astype(BF16)


def fresh_rows(new_ref, new_scr):
    prompts, new, _ = new_ref.shape
    new_scr[...] = jnp.zeros_like(new_scr)
    for prompt in range(prompts):
        new_scr[prompt * new : (prompt + 1) * new, :] = new_ref[prompt].astype(F32)


def tiles(width):
    for tile in range(width // (2 * LANES)):
        wide = slice(tile * 2 * LANES, (tile + 1) * 2 * LANES)
        thin = slice(tile * LANES, (tile + 1) * LANES)
        yield wide, thin


def sent_body(rows_ref, new_ref, w_ref, target_ref, send_ref, out_ref, new_scr):
    half = rows_ref.shape[0]
    w_rows = w_ref.shape[0]
    other = picker(1 - lax.axis_index("section"), w_rows)
    fresh_rows(new_ref, new_scr)
    for wide, thin in tiles(rows_ref.shape[1]):
        send_ref[:half, thin] = pick(rows_ref[:, wide], other)
        send_ref[half:, thin] = pick(new_scr[:, wide].astype(BF16), other)
    peers = out_ref.shape[0]
    targets = target_ref.shape[0]
    per_peer = targets // peers
    row = lax.broadcasted_iota(jnp.int32, (peers * SLOT, targets), 0)
    col = lax.broadcasted_iota(jnp.int32, (peers * SLOT, targets), 1)
    spread = one_hot((row % SLOT < per_peer) & (col == (row // SLOT) * per_peer + row % SLOT))
    slots = jnp.dot(spread, target_ref[...], preferred_element_type=F32)
    slots = slots.reshape(peers, SLOT, -1).astype(BF16)
    for peer in range(peers):
        out_ref[peer, :w_rows, :] = w_ref[...]
        out_ref[peer, w_rows:, :] = slots[peer]


def sent_half(rows, new_rows, w_value, target, replicas):
    row_count, width = rows.shape
    w_rows, columns = w_value.shape
    half = row_count // 2
    steps = 4
    block = width // steps
    sent = half + PAD
    return pl.pallas_call(
        sent_body,
        grid=(steps,),
        in_specs=[
            pl.BlockSpec((half, block), lambda i: (core_index(), i)),
            pl.BlockSpec((*new_rows.shape[:2], block), lambda i: (0, 0, i)),
            pl.BlockSpec((w_rows, columns), lambda i: (0, 0)),
            pl.BlockSpec((row_count // steps, columns), lambda i: (i, 0)),
        ],
        out_specs=[
            pl.BlockSpec((sent, block // 2), lambda i: (0, i)),
            pl.BlockSpec((replicas // steps, w_rows + SLOT, columns), lambda i: (i, 0, 0)),
        ],
        out_shape=[
            jax.ShapeDtypeStruct((sent, width // 2), BF16),
            jax.ShapeDtypeStruct((replicas, w_rows + SLOT, columns), BF16),
        ],
        cost_estimate=pl.CostEstimate(
            flops=2 * sent * width * LANES,
            bytes_accessed=4 * sent * width,
            transcendentals=0,
        ),
        scratch_shapes=[pltpu.VMEM((PAD, block), F32)],
        name="sent",
    )(rows, new_rows, w_value, target)


def kept_body(rows_ref, new_ref, keep_ref, new_scr, *, w_rows):
    row_count = rows_ref.shape[0]
    own = picker(lax.axis_index("section"), w_rows)
    fresh_rows(new_ref, new_scr)
    for wide, thin in tiles(rows_ref.shape[1]):
        keep_ref[:row_count, thin] = pick(rows_ref[:, wide], own)
        keep_ref[row_count:, thin] = pick(new_scr[:, wide].astype(BF16), own)


def kept_half(rows, new_rows, w_rows):
    row_count, width = rows.shape
    steps = 4
    block = width // steps
    kept = row_count + PAD
    return pl.pallas_call(
        lambda *refs: kept_body(*refs, w_rows=w_rows),
        grid=(steps,),
        in_specs=[
            pl.BlockSpec((row_count, block), lambda i: (0, i)),
            pl.BlockSpec((*new_rows.shape[:2], block), lambda i: (0, 0, i)),
        ],
        out_specs=pl.BlockSpec((kept, block // 2), lambda i: (0, i)),
        out_shape=jax.ShapeDtypeStruct((kept, width // 2), BF16),
        cost_estimate=pl.CostEstimate(
            flops=2 * kept * width * LANES,
            bytes_accessed=4 * kept * width,
            transcendentals=0,
        ),
        scratch_shapes=[pltpu.VMEM((PAD, block), F32)],
        compiler_params=pltpu.CompilerParams(vmem_limit_bytes=GRANT),
        name="kept",
    )(rows, new_rows)


VMEM = pl.BlockSpec(memory_space=pltpu.VMEM)


def theirs_body(first_ref, second_ref, block_ref, out_ref):
    core = core_index()
    peers, block_rows, columns = block_ref.shape
    w_rows = block_rows - SLOT
    half = first_ref.shape[0] - PAD
    weights = block_ref[:, :w_rows, :].reshape(peers * w_rows, columns)
    first_part = jnp.dot(first_ref[...], weights, preferred_element_type=F32)
    second_part = jnp.dot(second_ref[:half, :], weights, preferred_element_type=F32)
    near = pl.ds(pl.multiple_of(core * half, half), half)
    far = pl.ds(pl.multiple_of((1 - core) * half, half), half)
    out_ref[near, :] = first_part[:half]
    out_ref[far, :] = second_part
    out_ref[2 * half :, :] = first_part[half:]


def theirs_values(first, second, arrived):
    columns = arrived.shape[2]
    rows, width = first.shape
    return pl.pallas_call(
        theirs_body,
        in_specs=[VMEM] * 3,
        out_specs=VMEM,
        out_shape=jax.ShapeDtypeStruct((2 * rows - PAD, columns), F32),
        cost_estimate=pl.CostEstimate(
            flops=4 * width * columns * rows,
            bytes_accessed=2 * width * (2 * rows + columns),
            transcendentals=0,
        ),
        compiler_params=pltpu.CompilerParams(vmem_limit_bytes=GRANT),
        name="theirs",
    )(first, second, arrived)


def mine_body(kept_ref, block_ref, slot_ref, out_ref):
    peers, block_rows, columns = block_ref.shape
    w_rows = block_rows - SLOT
    row_count = kept_ref.shape[0] - PAD
    weights = block_ref[:, :w_rows, :].reshape(peers * w_rows, columns)
    slots = block_ref[:, w_rows:, :].reshape(peers * SLOT, columns)
    at = lax.broadcasted_iota(jnp.int32, (row_count, peers * SLOT), 0)
    place = one_hot(at == slot_ref[...])
    targets = jnp.dot(place, slots, preferred_element_type=F32)
    kept_part = jnp.dot(kept_ref[...], weights, preferred_element_type=F32)
    out_ref[:row_count, :] = kept_part[:row_count] - targets
    out_ref[row_count:, :] = kept_part[row_count:]


def mine_values(kept, arrived, slot_order):
    columns = arrived.shape[2]
    rows, width = kept.shape
    return pl.pallas_call(
        mine_body,
        in_specs=[VMEM] * 3,
        out_specs=VMEM,
        out_shape=jax.ShapeDtypeStruct((rows, columns), F32),
        cost_estimate=pl.CostEstimate(
            flops=2 * width * columns * rows,
            bytes_accessed=2 * width * (rows + columns),
            transcendentals=0,
        ),
        compiler_params=pltpu.CompilerParams(vmem_limit_bytes=GRANT),
        name="mine",
    )(kept, arrived, slot_order.reshape(1, -1))


def turn_body(kept_ref, first_ref, second_ref, out_ref):
    width, both = out_ref.shape
    row_count = both // 2
    half = row_count // 2
    block = 512
    for start in range(0, width, block):
        at = slice(start, start + block)
        out_ref[at, :row_count] = kept_ref[:row_count, at].T
        pair = jnp.concatenate([first_ref[:half, at], second_ref[:half, at]], axis=0)
        out_ref[at, row_count:] = pair.T


def turned(kept, first, second):
    width = kept.shape[1]
    row_count = kept.shape[0] - PAD
    return pl.pallas_call(
        turn_body,
        in_specs=[VMEM, VMEM, VMEM],
        out_specs=VMEM,
        out_shape=jax.ShapeDtypeStruct((width, 2 * row_count), BF16),
        cost_estimate=pl.CostEstimate(
            flops=0, bytes_accessed=8 * width * row_count, transcendentals=0
        ),
        compiler_params=pltpu.CompilerParams(vmem_limit_bytes=GRANT),
        name="turned",
    )(kept, first, second)


def product_body(rows_ref, mine_ref, theirs_ref, its_mine_ref, its_theirs_ref, out_ref):
    core = core_index()
    row_count = mine_ref.shape[0] - PAD
    half = row_count // 2
    own = (mine_ref[:row_count, :] + its_theirs_ref[:row_count, :]).astype(BF16)

    def residual(at):
        at = pl.ds(pl.multiple_of(at, half), half)
        return (theirs_ref[at, :] + its_mine_ref[at, :]).astype(BF16)

    residuals = [own, residual(core * half), residual((1 - core) * half)]
    residuals = jnp.concatenate(residuals, axis=0)
    out_ref[...] = jnp.dot(rows_ref[...], residuals, preferred_element_type=F32).astype(BF16)


def weight_product(rows, mine, theirs, its_mine, its_theirs):
    width, both = rows.shape
    columns = mine.shape[1]
    return pl.pallas_call(
        product_body,
        in_specs=[VMEM] * 5,
        out_specs=VMEM,
        out_shape=jax.ShapeDtypeStruct((width, columns), BF16),
        cost_estimate=pl.CostEstimate(
            flops=2 * width * columns * both,
            bytes_accessed=2 * width * (both + columns),
            transcendentals=0,
        ),
        compiler_params=pltpu.CompilerParams(vmem_limit_bytes=GRANT),
        name="product",
    )(rows, mine, theirs, its_mine, its_theirs)


def swap_section(x):
    return lax.ppermute(x, "section", [(0, 1), (1, 0)])


def swap_core(x):
    return lax.ppermute(x, "tensor", [(i, i ^ 1) for i in range(lax.axis_size("tensor"))])


def per_device(
    w_value,
    hidden_new,
    query,
    key_new,
    key_cache,
    value_cache,
    cache_len,
    sampled_rows,
    mb_map,
    value_target,
):
    replicas = lax.axis_size(DP)
    row_count = sampled_rows.shape[0]
    per_peer = row_count // replicas
    w_rows, width_local = w_value.shape
    prompts = hidden_new.shape[0]
    new_count = prompts * NEW
    slot_order = jnp.pad(
        mb_map[0].reshape(replicas, per_peer), ((0, 0), (0, SLOT - per_peer)), constant_values=-1
    )

    sent, outgoing = sent_half(sampled_rows, hidden_new, w_value, value_target, replicas)
    kept = kept_half(sampled_rows, hidden_new, w_rows)
    first = swap_section(sent)
    arrived = lax.all_to_all(outgoing, DP, 0, 0, tiled=True)
    second = swap_core(first)
    theirs = theirs_values(first, second, arrived)
    its_theirs = swap_section(theirs)
    mine = mine_values(kept, arrived, slot_order)
    its_mine = swap_section(mine)
    rows_turned = turned(kept, first, second)
    v_new_rows = (mine[row_count:] + its_theirs[row_count:])[:new_count]
    product = weight_product(rows_turned, mine, theirs, its_mine, its_theirs)
    terms = lax.all_to_all(
        product.reshape(replicas, w_rows, width_local), DP, 0, 0, tiled=True
    )
    grad_value = jnp.sum(terms.astype(jnp.float32) * (1.0 / row_count), axis=0)
    heads_local = width_local // HD
    cache_size = key_cache.shape[1]
    scale = 1.0 / jnp.sqrt(jnp.float32(HD))
    v_new = v_new_rows.astype(jnp.bfloat16).reshape(prompts, NEW, heads_local, HD)
    query_h = query.reshape(prompts, NEW, heads_local, QPK, HD)
    kc_heads = key_cache.reshape(prompts, cache_size, heads_local, HD)
    vc_heads = value_cache.reshape(prompts, cache_size, heads_local, HD)
    kn_heads = key_new.reshape(prompts, NEW, heads_local, HD)
    score_cache = (
        jnp.einsum("ptgqd,pjgd->pgtqj", query_h, kc_heads, preferred_element_type=jnp.float32)
        * scale
    )
    score_new = (
        jnp.einsum("ptgqd,pugd->pgtqu", query_h, kn_heads, preferred_element_type=jnp.float32)
        * scale
    )
    live_cache = (jnp.arange(cache_size)[None, :] < cache_len[:, None])[:, None, None, None, :]
    live_new = (jnp.arange(NEW)[None, :] <= jnp.arange(NEW)[:, None])[None, None, :, None, :]
    score_cache = jnp.where(live_cache, score_cache, -1e30)
    score_new = jnp.where(live_new, score_new, -1e30)
    peak = jnp.maximum(jnp.max(score_cache, axis=-1), jnp.max(score_new, axis=-1))[..., None]
    exp_cache = jnp.where(live_cache, jnp.exp(score_cache - peak), 0.0)
    exp_new = jnp.where(live_new, jnp.exp(score_new - peak), 0.0)
    total = jnp.sum(exp_cache, axis=-1, keepdims=True) + jnp.sum(exp_new, axis=-1, keepdims=True)
    prob_cache = (exp_cache / total).astype(jnp.bfloat16)
    prob_new = (exp_new / total).astype(jnp.bfloat16)
    mixed = jnp.einsum(
        "pgtqj,pjgd->ptgqd", prob_cache, vc_heads, preferred_element_type=jnp.float32
    )
    mixed = mixed + jnp.einsum(
        "pgtqu,pugd->ptgqd", prob_new, v_new, preferred_element_type=jnp.float32
    )
    attn_out = mixed.reshape(prompts, NEW, heads_local * QPK * HD).astype(jnp.bfloat16)
    return (attn_out, grad_value)


def solution(mesh):
    torus = Mesh(
        mesh.devices.reshape(8, 8, mesh.shape["tensor"], mesh.shape["section"]),
        ("dp_0", "dp_1", "tensor", "section"),
    )
    return jax.shard_map(
        per_device,
        mesh=torus,
        in_specs=(
            P(DP_SECTION, "tensor"),
            P(DP_SECTION, None, None),
            P(DP_SECTION, None, "tensor"),
            P(DP_SECTION, None, "tensor"),
            P(DP_SECTION, None, "tensor"),
            P(DP_SECTION, None, "tensor"),
            P(DP_SECTION),
            P(DP_SECTION, None),
            P(DP_SECTION, None),
            P(DP_SECTION, "tensor"),
        ),
        out_specs=(P(DP_SECTION, None, "tensor"), P(DP_SECTION, "tensor")),
        check_vma=False,
    )
```
